1024 devices in a mesh: bag: 64 (over z, core), head: 16 (over x, y).
Axes of the slice: x: 4, y: 4, z: 32, core: 2. Of those that a mesh axis runs over, the one named last changes fastest.
Arguments:
- projected: bfloat16 [131072, 3, 2048], P(('bag', 'head')), may hold values from -5.2 to 5.2
- video_ids: int32 [131072], P(('bag', 'head')), may hold values from 0 to 127, as said below
- bag_route: int32 [131072], P(('bag', 'head')), may hold values from 0 to 63, as said below
Outputs:
- attended: bfloat16 [131072, 2048], P(('bag', 'head'))
The draws below stay inside these ranges and needn't reach their ends.
Inputs may be any that keep to these rules, and one draw needn't show every extreme that they name: `bag_route`: every device's 128 tokens name each bag exactly 2 times, so every bag receives 2048 tokens. `video_ids`: all tokens of a video have the same bag_route; the tokens of bag b belong to exactly 2 videos, numbered b * 2 to b * 2 + 1.
All inputs are finite; a program needn't handle non-finite values.
Results may differ from the reference program's by a relative error of at most 0.0046.
Values may be sent and summed in bfloat16 or wider, within the bound.
A program may use at most 64 MiB of HBM per device.

```python
import math
import jax
import jax.numpy as jnp
from jax import lax

HEADS = 16
HD = 128
TOK_DEV = 128
VIDS_BAG = 2
PER_BAG = 2
BAG_ROWS = 2048
TOKENS = 131072


def make_plan(key):
    bags = TOKENS // BAG_ROWS
    all_devices = TOKENS // TOK_DEV
    cut_key, bag_key, device_key = jax.random.split(jax.random.fold_in(key, 101), 3)

    def video_cuts(sub_key):
        picks = jax.random.permutation(sub_key, BAG_ROWS - 1)[:VIDS_BAG - 1] + 1
        marks = jnp.zeros((BAG_ROWS,), jnp.int32).at[picks].set(1)
        return jnp.cumsum(marks).astype(jnp.int32)
    local_video = jax.vmap(video_cuts)(jax.random.split(cut_key, bags))
    video = local_video + jnp.arange(bags, dtype=jnp.int32)[:, None] * VIDS_BAG
    bag_perms = jax.vmap(lambda sub_key: jax.random.permutation(sub_key, BAG_ROWS))(jax.random.split(bag_key, bags))
    sorted_pos = jnp.transpose(bag_perms.reshape(bags, all_devices, PER_BAG), (1, 0, 2)).reshape(all_devices, TOK_DEV)
    device_perms = jax.vmap(lambda sub_key: jax.random.permutation(sub_key, TOK_DEV))(jax.random.split(device_key, all_devices))
    bag_home = (device_perms // PER_BAG).astype(jnp.int32)
    pos_home = jnp.take_along_axis(sorted_pos, device_perms, axis=1).astype(jnp.int32)
    route_rows = bag_home.reshape(TOKENS)
    id_rows = video[bag_home, pos_home].reshape(TOKENS)
    return (route_rows, id_rows)


def draw_bag_route(key, part):
    return make_plan(key)[0]


def draw_video_ids(key, part):
    return make_plan(key)[1]


def draw_projected(key, part):
    feature_width = HEADS * HD
    queries = jax.random.normal(jax.random.fold_in(key, 221), (TOKENS, feature_width), jnp.float32)
    key_part = jax.random.normal(jax.random.fold_in(key, 222), (TOKENS, feature_width), jnp.float32)
    value_part = jax.random.normal(jax.random.fold_in(key, 223), (TOKENS, feature_width), jnp.float32)
    queries = jnp.clip(queries, -5.0, 5.0)
    key_part = jnp.clip(key_part, -5.0, 5.0)
    value_part = jnp.clip(value_part, -5.0, 5.0)
    return jnp.stack([queries.astype(jnp.bfloat16), key_part.astype(jnp.bfloat16), value_part.astype(jnp.bfloat16)], axis=1)


def setup_inputs(seed: int = 0) -> dict:
    arg_keys = jax.random.split(jax.random.key(seed), 4)
    return {
        "projected": draw_projected(jax.random.fold_in(arg_keys[3], 71), 0),
        "video_ids": draw_video_ids(jax.random.fold_in(arg_keys[3], 71), 0),
        "bag_route": draw_bag_route(jax.random.fold_in(arg_keys[3], 71), 0),
    }


def attend_head(query_rows, key_rows, value_rows, row_ids):
    scaling = 1.0 / math.sqrt(HD)
    scores = jnp.dot(query_rows.astype(jnp.float32), key_rows.astype(jnp.float32).T) * scaling
    allowed = row_ids[:, None] == row_ids[None, :]
    scores = jnp.where(allowed, scores, -jnp.inf)
    row_max = lax.optimization_barrier(jnp.max(scores, axis=1, keepdims=True))
    weights = jnp.exp(scores - row_max)
    row_total = lax.optimization_barrier(jnp.sum(weights, axis=1, keepdims=True))
    rounded = lax.optimization_barrier(weights.astype(jnp.bfloat16))
    mixed_sum = jnp.dot(rounded.astype(jnp.float32), value_rows.astype(jnp.float32))
    return (mixed_sum / row_total).astype(jnp.bfloat16)

def reference(projected, video_ids, bag_route):
    bags = TOKENS // BAG_ROWS
    ordering = jnp.argsort(bag_route, stable=True)
    sorted_rows = projected[ordering].reshape(bags, BAG_ROWS, 3, HEADS, HD)
    sorted_ids = video_ids[ordering].reshape(bags, BAG_ROWS)

    def one_bag(inputs):
        bag_rows, row_ids = inputs
        heads_first = jnp.transpose(bag_rows, (2, 1, 0, 3))

        def one_head(stacked):
            return attend_head(stacked[0], stacked[1], stacked[2], row_ids)
        out_heads = lax.map(one_head, heads_first)
        return jnp.transpose(out_heads, (1, 0, 2)).reshape(BAG_ROWS, HEADS * HD)
    finished = lax.map(one_bag, (sorted_rows, sorted_ids)).reshape(TOKENS, HEADS * HD)
    return finished[jnp.argsort(ordering)]
```

```python
import functools
import math

import jax
import jax.numpy as jnp
from jax import lax
from jax.experimental import pallas as pl
from jax.experimental.pallas import tpu as pltpu
from jax.sharding import PartitionSpec as P

HD = 128
VIDEOS = 2
CHUNKS = 4
GROUP = 8
APART = 2.0**100
MESH = pl.DeviceIdType.MESH
F32, BF16, I32 = jnp.float32, jnp.bfloat16, jnp.int32


def reach(bag, slot, bags, way):
    chips = bags // 2
    hops = chips // 2 - lax.div(slot + 2, 4)
    side = way * (1 - 2 * lax.rem(lax.div(slot + 2, 2), 2))
    chip = lax.rem(lax.div(bag, 2) + hops * side + chips, chips)
    return chip * 2 + lax.rem(lax.rem(bag, 2) + slot + 1, 2)


def reach_rows(bag, slot, bags):
    chips = bags // 2
    hops = chips // 2 - ((slot + 2) >> 2)
    side = 1 - 2 * (((slot + 2) >> 1) & 1)
    chip = (lax.div(bag, 2) + hops * side + chips) & (chips - 1)
    return chip * 2 + ((lax.rem(bag, 2) + slot + 1) & 1)


def mat(a, b):
    return jnp.dot(a, b, preferred_element_type=F32)


def kernel(
    bags, heads, scaling,
    x_ref, ids_ref, route_ref, out_ref,
    place, place_t, mix, mix_t, picked,
    zs, zr, ys, kv, qs, qr, ka, va, qaug, oc, zos, zor, yo, home,
    bit_s, bit_r, row_s, row_r,
    zs_sem, zr_sem, zq_sem, zo_sem, xs_sem, xr_sem, xq_sem, xo_sem,
):
    bag, head = lax.axis_index("bag"), lax.axis_index("head")
    tok = x_ref.shape[1]
    last = bags - 1
    slots = bags // CHUNKS
    rows = 2 * slots
    span = 2 * GROUP
    pair = 2 * heads
    groups = slots // GROUP

    barrier = pltpu.get_barrier_semaphore()

    def greet_bag(k, carry):
        pl.semaphore_signal(
            barrier, inc=1, device_id=(reach(bag, k, bags, 1), head), device_id_type=MESH
        )
        return carry

    def greet_head(j, carry):
        pl.semaphore_signal(
            barrier, inc=1, device_id=(bag, lax.rem(head + 1 + j, heads)), device_id_type=MESH
        )
        return carry

    lax.fori_loop(0, last, greet_bag, 0)
    lax.fori_loop(0, heads - 1, greet_head, 0)

    route = route_ref[...]
    lanes = jnp.broadcast_to(route.astype(F32), (tok, tok))
    down = lax.broadcasted_iota(I32, (tok, tok), 0)
    along = lax.broadcasted_iota(I32, (tok, tok), 1)
    earlier = (lanes == lanes.T) & (down < along)
    rank = jnp.sum(jnp.where(earlier, 1.0, 0.0), axis=0, keepdims=True).astype(I32)
    hit = (reach_rows(bag, down >> 1, bags) == route) & (rank == (down & 1))
    spots = jnp.where(hit, 1.0, 0.0)
    place[...] = spots.astype(BF16)
    place_t[...] = spots.T.astype(BF16)

    side = mix.shape[0]
    mo = lax.broadcasted_iota(I32, (side, side), 0)
    mi = lax.broadcasted_iota(I32, (side, side), 1)
    h_bits = heads.bit_length() - 1

    def swapped(a):
        head_of, slot_of, pair_of = a >> 4, (a >> 1) & (GROUP - 1), a & 1
        return (slot_of << (h_bits + 1)) + head_of * 2 + pair_of

    mix[...] = jnp.where(swapped(mo) == mi, 1.0, 0.0).astype(BF16)
    mix_t[...] = jnp.where(swapped(mi) == mo, 1.0, 0.0).astype(BF16)

    slot_rows = lax.broadcasted_iota(I32, (bags, tok), 0)
    bits = (ids_ref[...] - VIDEOS * route).astype(F32)
    mine = jnp.where(reach_rows(bag, slot_rows, bags) == route, bits, 0.0)
    pick = jnp.where(rank == down, 1.0, 0.0)
    slot_bits = lax.dot_general(
        mine.astype(BF16), pick.astype(BF16), (((1,), (1,)), ((), ())), preferred_element_type=F32
    )
    bit_s[...] = slot_bits.reshape(bags, 1, tok)

    def split(i, carry):
        t = lax.rem(i + 1, 3)
        picked[...] = mat(place[...], x_ref[t]).astype(BF16)
        for g in range(bags // GROUP):
            block = jnp.concatenate(
                [picked[g * span : (g + 1) * span, h * HD : (h + 1) * HD] for h in range(heads)],
                axis=0,
            )
            spread = mat(mix_t[...], block).astype(BF16)
            zs[t, g * GROUP : (g + 1) * GROUP] = spread.reshape(GROUP, pair, HD)
        return carry

    lax.fori_loop(0, 3, split, 0)

    pl.semaphore_wait(barrier, last + heads - 1)

    def across(k, src, dst, send, recv, way):
        pltpu.make_async_remote_copy(
            src_ref=src, dst_ref=dst, send_sem=send, recv_sem=recv,
            device_id=(reach(bag, k, bags, way), head), device_id_type=MESH,
        ).start()

    def send_tensor(t, recv, lo, hi):
        def one(k, carry):
            across(k, zs.at[t, k], zr.at[t, k], zs_sem.at[t], recv, 1)
            return carry

        lax.fori_loop(lo, hi, one, 0)

    def send_bits(k, carry):
        across(k, bit_s.at[k], bit_r.at[k], zs_sem.at[3], zr_sem.at[2], 1)
        return carry

    def keep(src, dst, sem):
        pltpu.make_async_copy(src, dst, sem).start()

    def arrived(ref, sem):
        pltpu.make_async_copy(ref, ref, sem).wait()

    send_tensor(1, zr_sem.at[0], 0, last)
    keep(zs.at[1, last], zr.at[1, last], zr_sem.at[0])
    lax.fori_loop(0, last, send_bits, 0)
    keep(bit_s.at[last], bit_r.at[last], zr_sem.at[2])
    send_tensor(2, zr_sem.at[1], 0, last)
    keep(zs.at[2, last], zr.at[2, last], zr_sem.at[1])

    def send_queries(c, carry):
        send_tensor(0, zq_sem.at[c], c * slots, (c + 1) * slots - lax.div(c, CHUNKS - 1))
        return carry

    lax.fori_loop(0, CHUNKS, send_queries, 0)
    keep(zs.at[0, last], zr.at[0, last], zq_sem.at[CHUNKS - 1])

    def hand_out(src, dst, send, recv):
        def one(j, carry):
            to = lax.rem(head + 1 + j, heads)
            pltpu.make_async_remote_copy(
                src_ref=src(to), dst_ref=dst, send_sem=send, recv_sem=recv,
                device_id=(bag, to), device_id_type=MESH,
            ).start()
            return carry

        lax.fori_loop(0, heads - 1, one, 0)
        keep(src(head), dst, recv)

    def gather_kv(i):
        for g in range(bags // GROUP):
            block = zr[1 + i, g * GROUP : (g + 1) * GROUP].reshape(side, HD)
            ys[i, :, g * span : (g + 1) * span, :] = (
                mat(mix[...], block).astype(BF16).reshape(heads, span, HD)
            )
        hand_out(lambda to: ys.at[i, to], kv.at[i, head], xs_sem.at[1 + i], xr_sem.at[i])

    arrived(zr.at[1], zr_sem.at[0])
    gather_kv(0)

    arrived(bit_r, zr_sem.at[2])
    got = bit_r[...].reshape(bags, tok)
    lane = lax.broadcasted_iota(I32, (bags, tok), 1)
    spread_bits = jnp.where((lane & 1) == 0, got[:, 0:1], got[:, 1:2])
    own = lax.broadcasted_iota(I32, (bags, tok), 0) == (lane >> 1)
    row_s[...] = jnp.sum(jnp.where(own, spread_bits, 0.0), axis=0, keepdims=True)
    hand_out(lambda to: row_s, row_r.at[head], xs_sem.at[3], xr_sem.at[2])

    arrived(row_r, xr_sem.at[2])
    columns = row_r[...].reshape(heads, tok).T
    lane_row = lax.broadcasted_iota(I32, (1, HD), 1)
    first, second = lane_row == 0, lane_row == 1
    q_slope = jnp.where(first, 1.0, jnp.where(second, -1.0, 0.0))
    q_base = jnp.where(second, 1.0, 0.0)
    k_slope = q_slope * APART
    k_base = jnp.where(first, -APART, 0.0)
    for h in range(heads):
        column = columns[:, h : h + 1]
        qaug[:, h] = (column * q_slope + q_base).astype(BF16).reshape(CHUNKS, rows, HD)
        ka[h * tok : (h + 1) * tok, HD:] = (column * k_slope + k_base).astype(BF16)

    arrived(kv.at[0], xr_sem.at[0])
    ka[:, :HD] = kv[0].reshape(heads * tok, HD)

    arrived(zr.at[2], zr_sem.at[1])
    gather_kv(1)
    va[:, HD:] = jnp.broadcast_to(jnp.where(first, 1.0, 0.0), (heads * tok, HD)).astype(BF16)
    arrived(kv.at[1], xr_sem.at[1])
    va[:, :HD] = kv[1].reshape(heads * tok, HD)

    part = GROUP
    exponent = scaling * math.log2(math.e)

    def answer(c, carry):
        base = pl.multiple_of(c * slots, slots)
        arrived(zr.at[0, pl.ds(base, slots)], zq_sem.at[c])
        for j in range(groups):
            block = zr[0, pl.ds(base + j * GROUP, GROUP)].reshape(side, HD)
            qs[c, :, j * span : (j + 1) * span, :] = (
                mat(mix[...], block).astype(BF16).reshape(heads, span, HD)
            )
        hand_out(lambda to: qs.at[c, to], qr.at[c, head], xs_sem.at[0], xq_sem.at[c])
        arrived(qr.at[c], xq_sem.at[c])

        def block_of(i, inner):
            at = pl.ds(i * part, part)
            query = jnp.concatenate(
                [qr[c, at].reshape(part * rows, HD), qaug[c, at].reshape(part * rows, HD)], axis=1
            )
            scores = lax.dot_general(
                query, ka[...], (((1,), (1,)), ((), ())), preferred_element_type=F32
            )
            row_max = jnp.max(scores, axis=1, keepdims=True)
            probs = jnp.exp2((scores - row_max) * exponent).astype(BF16)
            mixed = mat(probs, va[...])
            result = (mixed[:, :HD] / mixed[:, HD : HD + 1]).astype(BF16)
            oc[at] = result.reshape(part, rows, HD)
            return inner

        lax.fori_loop(0, heads // part, block_of, 0)
        for j in range(groups):
            block = oc[:, j * span : (j + 1) * span, :].reshape(side, HD)
            zos[pl.ds(base + j * GROUP, GROUP)] = (
                mat(mix_t[...], block).astype(BF16).reshape(GROUP, pair, HD)
            )

        def give_back(k, inner):
            across(k, zos.at[k], zor.at[k], zs_sem.at[4], zo_sem.at[c], -1)
            return inner

        lax.fori_loop(c * slots, (c + 1) * slots - lax.div(c, CHUNKS - 1), give_back, 0)
        return carry

    lax.fori_loop(0, CHUNKS, answer, 0)
    keep(zos.at[last], zor.at[last], zo_sem.at[CHUNKS - 1])

    def collect(c, carry):
        base = pl.multiple_of(c * slots, slots)
        arrived(zor.at[pl.ds(base, slots)], zo_sem.at[c])
        for j in range(groups):
            block = zor[pl.ds(base + j * GROUP, GROUP)].reshape(side, HD)
            yo[c, :, j * span : (j + 1) * span, :] = (
                mat(mix[...], block).astype(BF16).reshape(heads, span, HD)
            )
        hand_out(
            lambda to: yo.at[c, to],
            home.at[c, :, pl.ds(pl.multiple_of(head * HD, HD), HD)],
            xs_sem.at[4],
            xo_sem.at[c],
        )
        return carry

    lax.fori_loop(0, CHUNKS, collect, 0)

    def landed(c, carry):
        arrived(home.at[c], xo_sem.at[c])
        return carry

    lax.fori_loop(0, CHUNKS, landed, 0)
    out_ref[...] = mat(place_t[...], home[...].reshape(tok, heads * HD)).astype(BF16)

    for t in range(3):
        arrived(zs.at[t, pl.ds(0, last)], zs_sem.at[t])
    arrived(bit_s.at[pl.ds(0, last)], zs_sem.at[3])
    arrived(zos.at[pl.ds(0, last)], zs_sem.at[4])
    arrived(qs.at[:, pl.ds(0, heads - 1)], xs_sem.at[0])
    for i in range(2):
        arrived(ys.at[i, pl.ds(0, heads - 1)], xs_sem.at[1 + i])
    arrived(row_r.at[pl.ds(0, heads - 1)], xs_sem.at[3])
    arrived(yo.at[:, pl.ds(0, heads - 1)], xs_sem.at[4])


def local(bags, heads, projected, video_ids, bag_route):
    tok, _, feat = projected.shape
    slots = bags // CHUNKS
    rows = 2 * slots
    bag_rows = heads * tok
    side = GROUP * 2 * heads
    vm, dma = pltpu.VMEM, pltpu.SemaphoreType.DMA
    return pl.pallas_call(
        functools.partial(kernel, bags, heads, 1.0 / math.sqrt(HD)),
        out_shape=jax.ShapeDtypeStruct((tok, feat), BF16),
        in_specs=[pl.BlockSpec(memory_space=pltpu.VMEM)] * 3,
        out_specs=pl.BlockSpec(memory_space=pltpu.VMEM),
        scratch_shapes=[
            vm((tok, tok), BF16),
            vm((tok, tok), BF16),
            vm((side, side), BF16),
            vm((side, side), BF16),
            vm((tok, feat), BF16),
            vm((3, bags, 2 * heads, HD), BF16),
            vm((3, bags, 2 * heads, HD), BF16),
            vm((2, heads, tok, HD), BF16),
            vm((2, heads, tok, HD), BF16),
            vm((CHUNKS, heads, rows, HD), BF16),
            vm((CHUNKS, heads, rows, HD), BF16),
            vm((bag_rows, 2 * HD), BF16),
            vm((bag_rows, 2 * HD), BF16),
            vm((CHUNKS, heads, rows, HD), BF16),
            vm((heads, rows, HD), BF16),
            vm((bags, 2 * heads, HD), BF16),
            vm((bags, 2 * heads, HD), BF16),
            vm((CHUNKS, heads, rows, HD), BF16),
            vm((CHUNKS, rows, feat), BF16),
            vm((bags, 1, tok), F32),
            vm((bags, 1, tok), F32),
            vm((1, tok), F32),
            vm((heads, 1, tok), F32),
            dma((5,)),
            dma((3,)),
            dma((CHUNKS,)),
            dma((CHUNKS,)),
            dma((5,)),
            dma((3,)),
            dma((CHUNKS,)),
            dma((CHUNKS,)),
        ],
        compiler_params=pltpu.CompilerParams(
            collective_id=0, has_side_effects=True, vmem_limit_bytes=48 << 20
        ),
        name="routed_attention",
    )(jnp.transpose(projected, (1, 0, 2)), video_ids.reshape(1, tok), bag_route.reshape(1, tok))


def solution(mesh):
    placed = (P(("bag", "head"), None, None), P(("bag", "head")), P(("bag", "head")))
    return jax.shard_map(
        functools.partial(local, mesh.shape["bag"], mesh.shape["head"]),
        mesh=mesh,
        in_specs=placed,
        out_specs=P(("bag", "head"), None),
        check_vma=False,
    )
```

```python
import functools
import math

import jax
import jax.numpy as jnp
from jax import lax
from jax.experimental import pallas as pl
from jax.experimental.pallas import tpu as pltpu
from jax.sharding import PartitionSpec as P

HD = 128
VIDEOS = 2
CHUNKS = 4
GROUP = 8
APART = 2.0**100
MESH = pl.DeviceIdType.MESH
F32, BF16, I32 = jnp.float32, jnp.bfloat16, jnp.int32


def reach(bag, slot, bags, way):
    chips = bags // 2
    hops = chips // 2 - lax.div(slot + 2, 4)
    side = way * (1 - 2 * lax.rem(lax.div(slot + 2, 2), 2))
    chip = lax.rem(lax.div(bag, 2) + hops * side + chips, chips)
    return chip * 2 + lax.rem(lax.rem(bag, 2) + slot + 1, 2)


def reach_rows(bag, slot, bags):
    chips = bags // 2
    hops = chips // 2 - ((slot + 2) >> 2)
    side = 1 - 2 * (((slot + 2) >> 1) & 1)
    chip = (lax.div(bag, 2) + hops * side + chips) & (chips - 1)
    return chip * 2 + ((lax.rem(bag, 2) + slot + 1) & 1)


def mat(a, b):
    return jnp.dot(a, b, preferred_element_type=F32)


def kernel(
    bags, heads, scaling,
    x_hbm, ids_hbm, route_hbm, out_ref,
    x_ref, ids_ref, route_ref,
    place, place_t, mix, mix_t, picked,
    zs, zr, ys, kv, qs, qr, ka, va, qaug, oc, oc_in, zos, zor, home,
    row_s, row_r, bit_s, bit_r, all_bits,
    zs_sem, zr_sem, zq_sem, zo_sem, xs_sem, xr_sem, xq_sem, xo_sem, in_sem, wave,
):
    bag, head = lax.axis_index("bag"), lax.axis_index("head")
    tok = x_ref.shape[1]
    last = bags - 1
    slots = bags // CHUNKS
    rows = 2 * slots
    span = 2 * GROUP
    pair = 2 * heads
    groups = slots // GROUP

    chips = bags // 2
    chip, core = lax.div(bag, 2), lax.rem(bag, 2)
    above, below = lax.rem(chip + 1, chips) * 2, lax.rem(chip + chips - 1, chips) * 2

    barrier = pltpu.get_barrier_semaphore()

    def greet(to_bag, to_head):
        pl.semaphore_signal(barrier, inc=1, device_id=(to_bag, to_head), device_id_type=MESH)

    for near in (above, below):
        greet(near, head)
        greet(near + 1, head)
    greet(chip * 2 + 1 - core, head)
    for j in range(1, heads):
        greet(bag, lax.rem(head + j, heads))

    loads = [
        pltpu.make_async_copy(route_hbm, route_ref, in_sem.at[3]),
        pltpu.make_async_copy(ids_hbm, ids_ref, in_sem.at[4]),
    ] + [pltpu.make_async_copy(x_hbm.at[t], x_ref.at[t], in_sem.at[t]) for t in (1, 2, 0)]
    for load in loads:
        load.start()
    loads[0].wait()
    loads[1].wait()

    route = route_ref[...]
    lanes = jnp.broadcast_to(route.astype(F32), (tok, tok))
    down = lax.broadcasted_iota(I32, (tok, tok), 0)
    along = lax.broadcasted_iota(I32, (tok, tok), 1)
    earlier = (lanes == lanes.T) & (down < along)
    rank = jnp.sum(jnp.where(earlier, 1.0, 0.0), axis=0, keepdims=True).astype(I32)
    hit = (reach_rows(bag, down >> 1, bags) == route) & (rank == (down & 1))
    spots = jnp.where(hit, 1.0, 0.0)
    place[...] = spots.astype(BF16)
    place_t[...] = spots.T.astype(BF16)

    side = mix.shape[0]
    mo = lax.broadcasted_iota(I32, (side, side), 0)
    mi = lax.broadcasted_iota(I32, (side, side), 1)
    h_bits = heads.bit_length() - 1

    def swapped(a):
        head_of, slot_of, pair_of = a >> 4, (a >> 1) & (GROUP - 1), a & 1
        return (slot_of << (h_bits + 1)) + head_of * 2 + pair_of

    mix[...] = jnp.where(swapped(mo) == mi, 1.0, 0.0).astype(BF16)
    mix_t[...] = jnp.where(swapped(mi) == mo, 1.0, 0.0).astype(BF16)

    bits = (ids_ref[...] - VIDEOS * route).astype(F32)
    row_s[...] = mat(jnp.broadcast_to(bits, (8, tok)).astype(BF16), place_t[...])[0:1]

    def split(t):
        pltpu.make_async_copy(x_hbm.at[t], x_ref.at[t], in_sem.at[t]).wait()
        picked[...] = mat(place[...], x_ref[t]).astype(BF16)

        def spread(g, carry):
            lines = pl.ds(pl.multiple_of(g * span, span), span)
            block = jnp.concatenate(
                [picked[lines, h * HD : (h + 1) * HD] for h in range(heads)], axis=0
            )
            zs[t, pl.ds(g * GROUP, GROUP)] = (
                mat(mix_t[...], block).astype(BF16).reshape(GROUP, pair, HD)
            )
            return carry

        lax.fori_loop(0, bags // GROUP, spread, 0, unroll=4)

    split(1)
    pl.semaphore_wait(barrier, 5 + heads - 1)

    def across(k, src, dst, send, recv, way):
        pltpu.make_async_remote_copy(
            src_ref=src, dst_ref=dst, send_sem=send, recv_sem=recv,
            device_id=(reach(bag, k, bags, way), head), device_id_type=MESH,
        ).start()

    def send_tensor(t, recv, lo, hi):
        def one(k, carry):
            across(k, zs.at[t, k], zr.at[t, k], zs_sem.at[t], recv, 1)
            return carry

        lax.fori_loop(lo, hi, one, 0)

    def keep(src, dst, sem):
        pltpu.make_async_copy(src, dst, sem).start()

    def arrived(ref, sem):
        pltpu.make_async_copy(ref, ref, sem).wait()

    def hand_out(src, dst, send, recv):
        def one(j, carry):
            to = lax.rem(head + 1 + j, heads)
            pltpu.make_async_remote_copy(
                src_ref=src(to), dst_ref=dst, send_sem=send, recv_sem=recv,
                device_id=(bag, to), device_id_type=MESH,
            ).start()
            return carry

        lax.fori_loop(0, heads - 1, one, 0)
        keep(src(head), dst, recv)

    hand_out(lambda to: row_s, row_r.at[head], xs_sem.at[3], xr_sem.at[2])

    send_tensor(1, zr_sem.at[0], last - 1, last)

    def widen(stage, carry):
        first_slot = 4 * (chips // 2 - stage) - 2
        for i in range(4):
            k = first_slot + i
            across(k, zs.at[1, k], zr.at[1, k], zs_sem.at[1], zr_sem.at[0], 1)
        for i, near in enumerate((below, above)):
            pl.semaphore_signal(
                wave.at[i], inc=1, device_id=(near + core, head), device_id_type=MESH
            )
        pl.semaphore_wait(wave.at[0], 1)
        pl.semaphore_wait(wave.at[1], 1)
        return carry

    lax.fori_loop(1, chips // 2, widen, 0)
    send_tensor(1, zr_sem.at[0], 0, 2)
    keep(zs.at[1, last], zr.at[1, last], zr_sem.at[0])

    share = bags // heads
    arrived(row_r, xr_sem.at[2])
    rows_in = row_r[...].reshape(heads, tok)
    odd = lax.broadcasted_iota(I32, (heads, tok), 1) & 1
    stacked = jnp.concatenate(
        [
            jnp.where(odd == 0, rows_in, 0.0),
            jnp.where(odd == 1, rows_in, 0.0),
            jnp.zeros((tok - 2 * heads, tok), F32),
        ],
        axis=0,
    )
    slot_at = lax.broadcasted_iota(I32, (bags, tok), 0)
    lane_at = lax.broadcasted_iota(I32, (bags, tok), 1)
    fold = jnp.where(slot_at == (lane_at >> 1), 1.0, 0.0)
    slot_bits = lax.dot_general(
        fold.astype(BF16), stacked.astype(BF16), (((1,), (1,)), ((), ())), preferred_element_type=F32
    )
    bit_s[...] = slot_bits.reshape(bags, 1, tok)

    def send_bits(j, carry):
        k = head + heads * j
        across(k, bit_s.at[k], bit_r.at[j], zs_sem.at[3], zr_sem.at[2], 1)
        return carry

    lax.fori_loop(0, share - 1, send_bits, 0)

    @pl.when(head < heads - 1)
    def _():
        send_bits(share - 1, 0)

    @pl.when(head == heads - 1)
    def _():
        keep(bit_s.at[last], bit_r.at[share - 1], zr_sem.at[2])

    split(2)
    send_tensor(2, zr_sem.at[1], 0, last)
    keep(zs.at[2, last], zr.at[2, last], zr_sem.at[1])
    split(0)

    def send_queries(c, carry):
        send_tensor(0, zq_sem.at[c], c * slots, (c + 1) * slots - lax.div(c, CHUNKS - 1))
        return carry

    lax.fori_loop(0, CHUNKS, send_queries, 0)
    keep(zs.at[0, last], zr.at[0, last], zq_sem.at[CHUNKS - 1])

    def gather_kv(i):
        for g in range(bags // GROUP):
            block = zr[1 + i, g * GROUP : (g + 1) * GROUP].reshape(side, HD)
            ys[i, :, g * span : (g + 1) * span, :] = (
                mat(mix[...], block).astype(BF16).reshape(heads, span, HD)
            )
        hand_out(lambda to: ys.at[i, to], kv.at[i, head], xs_sem.at[1 + i], xr_sem.at[i])

    arrived(zr.at[1], zr_sem.at[0])
    gather_kv(0)

    arrived(bit_r, zr_sem.at[2])
    hand_out(
        lambda to: bit_r, all_bits.at[pl.ds(head * share, share)], xs_sem.at[5], xr_sem.at[3]
    )
    arrived(all_bits, xr_sem.at[3])
    row_at = lax.broadcasted_iota(I32, (tok, bags), 0)
    from_at = lax.broadcasted_iota(I32, (tok, bags), 1)
    s_bits = share.bit_length() - 1
    named = (from_at >> s_bits) + heads * (from_at & (share - 1))
    wide = mat(
        jnp.where(named == (row_at >> 1), 1.0, 0.0).astype(BF16),
        all_bits[...].reshape(bags, tok).astype(BF16),
    )
    even = (lax.broadcasted_iota(I32, (tok, heads), 0) & 1) == 0
    columns = jnp.where(even, wide[:, :heads], wide[:, heads : 2 * heads])
    lane_row = lax.broadcasted_iota(I32, (1, HD), 1)
    first, second = lane_row == 0, lane_row == 1
    q_slope = jnp.where(first, 1.0, jnp.where(second, -1.0, 0.0))
    q_base = jnp.where(second, 1.0, 0.0)
    k_slope = q_slope * APART
    k_base = jnp.where(first, -APART, 0.0)
    for h in range(heads):
        column = columns[:, h : h + 1]
        qaug[:, h] = (column * q_slope + q_base).astype(BF16).reshape(CHUNKS, rows, HD)
        ka[h * tok : (h + 1) * tok, HD:] = (column * k_slope + k_base).astype(BF16)

    arrived(kv.at[0], xr_sem.at[0])
    ka[:, :HD] = kv[0].reshape(heads * tok, HD)

    arrived(zr.at[2], zr_sem.at[1])
    gather_kv(1)
    va[:, HD:] = jnp.broadcast_to(jnp.where(first, 1.0, 0.0), (heads * tok, HD)).astype(BF16)
    arrived(kv.at[1], xr_sem.at[1])
    va[:, :HD] = kv[1].reshape(heads * tok, HD)

    part = GROUP
    exponent = scaling * math.log2(math.e)

    def answer(c, carry):
        base = pl.multiple_of(c * slots, slots)
        arrived(zr.at[0, pl.ds(base, slots)], zq_sem.at[c])
        for j in range(groups):
            block = zr[0, pl.ds(base + j * GROUP, GROUP)].reshape(side, HD)
            qs[c, :, j * span : (j + 1) * span, :] = (
                mat(mix[...], block).astype(BF16).reshape(heads, span, HD)
            )
        hand_out(lambda to: qs.at[c, to], qr.at[c, head], xs_sem.at[0], xq_sem.at[c])
        arrived(qr.at[c], xq_sem.at[c])

        def block_of(i, inner):
            at = pl.ds(i * part, part)
            query = jnp.concatenate(
                [qr[c, at].reshape(part * rows, HD), qaug[c, at].reshape(part * rows, HD)], axis=1
            )
            scores = lax.dot_general(
                query, ka[...], (((1,), (1,)), ((), ())), preferred_element_type=F32
            )
            row_max = jnp.max(scores, axis=1, keepdims=True)
            probs = jnp.exp2((scores - row_max) * exponent).astype(BF16)
            mixed = mat(probs, va[...])
            result = (mixed[:, :HD] / mixed[:, HD : HD + 1]).astype(BF16)
            oc[c, at] = result.reshape(part, rows, HD)
            return inner

        lax.fori_loop(0, heads // part, block_of, 0)
        hand_out(lambda to: oc.at[c, to], oc_in.at[c, head], xs_sem.at[4], xo_sem.at[c])
        arrived(oc_in.at[c], xo_sem.at[c])
        for j in range(groups):
            block = oc_in[c, :, j * span : (j + 1) * span, :].reshape(side, HD)
            zos[pl.ds(base + j * GROUP, GROUP)] = (
                mat(mix_t[...], block).astype(BF16).reshape(GROUP, pair, HD)
            )

        def give_back(k, inner):
            across(k, zos.at[k], zor.at[k], zs_sem.at[4], zo_sem.at[c], -1)
            return inner

        lax.fori_loop(c * slots, (c + 1) * slots - lax.div(c, CHUNKS - 1), give_back, 0)
        return carry

    lax.fori_loop(0, CHUNKS, answer, 0)
    keep(zos.at[last], zor.at[last], zo_sem.at[CHUNKS - 1])

    def collect(c, carry):
        base = pl.multiple_of(c * slots, slots)
        arrived(zor.at[pl.ds(base, slots)], zo_sem.at[c])
        for j in range(groups):
            block = zor[pl.ds(base + j * GROUP, GROUP)].reshape(side, HD)
            sorted_rows = mat(mix[...], block).astype(BF16)
            for h in range(heads):
                home[c, j * span : (j + 1) * span, h * HD : (h + 1) * HD] = sorted_rows[
                    h * span : (h + 1) * span
                ]
        return carry

    lax.fori_loop(0, CHUNKS, collect, 0)
    out_ref[...] = mat(place_t[...], home[...].reshape(tok, heads * HD)).astype(BF16)

    for t in range(3):
        arrived(zs.at[t, pl.ds(0, last)], zs_sem.at[t])
    arrived(bit_s.at[pl.ds(0, share - 1)], zs_sem.at[3])

    @pl.when(head < heads - 1)
    def _():
        arrived(bit_s.at[last], zs_sem.at[3])

    arrived(zos.at[pl.ds(0, last)], zs_sem.at[4])
    arrived(qs.at[:, pl.ds(0, heads - 1)], xs_sem.at[0])
    for i in range(2):
        arrived(ys.at[i, pl.ds(0, heads - 1)], xs_sem.at[1 + i])
    arrived(row_r.at[pl.ds(0, heads - 1)], xs_sem.at[3])
    arrived(all_bits.at[pl.ds(0, bags - share)], xs_sem.at[5])
    arrived(oc.at[:, pl.ds(0, heads - 1)], xs_sem.at[4])


def local(bags, heads, projected, video_ids, bag_route):
    tok, _, feat = projected.shape
    slots = bags // CHUNKS
    rows = 2 * slots
    bag_rows = heads * tok
    side = GROUP * 2 * heads
    vm, dma = pltpu.VMEM, pltpu.SemaphoreType.DMA
    return pl.pallas_call(
        functools.partial(kernel, bags, heads, 1.0 / math.sqrt(HD)),
        out_shape=jax.ShapeDtypeStruct((tok, feat), BF16),
        in_specs=[pl.BlockSpec(memory_space=pltpu.HBM)] * 3,
        out_specs=pl.BlockSpec(memory_space=pltpu.VMEM),
        scratch_shapes=[
            vm((3, tok, feat), BF16),
            vm((1, tok), I32),
            vm((1, tok), I32),
            vm((tok, tok), BF16),
            vm((tok, tok), BF16),
            vm((side, side), BF16),
            vm((side, side), BF16),
            vm((tok, feat), BF16),
            vm((3, bags, 2 * heads, HD), BF16),
            vm((3, bags, 2 * heads, HD), BF16),
            vm((2, heads, tok, HD), BF16),
            vm((2, heads, tok, HD), BF16),
            vm((CHUNKS, heads, rows, HD), BF16),
            vm((CHUNKS, heads, rows, HD), BF16),
            vm((bag_rows, 2 * HD), BF16),
            vm((bag_rows, 2 * HD), BF16),
            vm((CHUNKS, heads, rows, HD), BF16),
            vm((CHUNKS, heads, rows, HD), BF16),
            vm((CHUNKS, heads, rows, HD), BF16),
            vm((bags, 2 * heads, HD), BF16),
            vm((bags, 2 * heads, HD), BF16),
            vm((CHUNKS, rows, feat), BF16),
            vm((1, tok), F32),
            vm((heads, 1, tok), F32),
            vm((bags, 1, tok), F32),
            vm((bags // heads, 1, tok), F32),
            vm((bags, 1, tok), F32),
            dma((5,)),
            dma((3,)),
            dma((CHUNKS,)),
            dma((CHUNKS,)),
            dma((6,)),
            dma((4,)),
            dma((CHUNKS,)),
            dma((CHUNKS,)),
            dma((5,)),
            pltpu.SemaphoreType.REGULAR((2,)),
        ],
        compiler_params=pltpu.CompilerParams(collective_id=0, has_side_effects=True),
        name="routed_attention",
    )(jnp.transpose(projected, (1, 0, 2)), video_ids.reshape(1, tok), bag_route.reshape(1, tok))


def solution(mesh):
    placed = (P(("bag", "head"), None, None), P(("bag", "head")), P(("bag", "head")))
    return jax.shard_map(
        functools.partial(local, mesh.shape["bag"], mesh.shape["head"]),
        mesh=mesh,
        in_specs=placed,
        out_specs=P(("bag", "head"), None),
        check_vma=False,
    )
```

```python
import functools
import math

import jax
import jax.numpy as jnp
from jax import lax
from jax.experimental import pallas as pl
from jax.experimental.pallas import tpu as pltpu
from jax.sharding import PartitionSpec as P

HD = 128
VIDEOS = 2
CHUNKS = 4
GROUP = 8
APART = 2.0**100
MESH = pl.DeviceIdType.MESH
F32, BF16, I32 = jnp.float32, jnp.bfloat16, jnp.int32


def reach(bag, slot, bags, way):
    chips = bags // 2
    hops = chips // 2 - lax.div(slot + 2, 4)
    side = way * (1 - 2 * lax.rem(lax.div(slot + 2, 2), 2))
    chip = lax.rem(lax.div(bag, 2) + hops * side + chips, chips)
    return chip * 2 + lax.rem(lax.rem(bag, 2) + slot + 1, 2)


def reach_rows(bag, slot, bags):
    chips = bags // 2
    hops = chips // 2 - ((slot + 2) >> 2)
    side = 1 - 2 * (((slot + 2) >> 1) & 1)
    chip = (lax.div(bag, 2) + hops * side + chips) & (chips - 1)
    return chip * 2 + ((lax.rem(bag, 2) + slot + 1) & 1)


def mat(a, b):
    return jnp.dot(a, b, preferred_element_type=F32)


def kernel(
    bags, heads, scaling,
    x_hbm, ids_hbm, route_hbm, home, place_out,
    x_ref, ids_ref, route_ref,
    place, place_t, mix, mix_t, picked,
    zs, zr, ys, kv, qs, qr, ka, va, qaug, oc, oc_in, zos, zor,
    row_s, row_r, bit_s, bit_r, all_bits,
    zs_sem, zr_sem, zq_sem, zo_sem, xs_sem, xr_sem, xq_sem, xo_sem, in_sem, wave,
):
    bag, head = lax.axis_index("bag"), lax.axis_index("head")
    tok = x_ref.shape[1]
    last = bags - 1
    slots = bags // CHUNKS
    rows = 2 * slots
    span = 2 * GROUP
    pair = 2 * heads
    groups = slots // GROUP

    chips = bags // 2
    chip, core = lax.div(bag, 2), lax.rem(bag, 2)
    above, below = lax.rem(chip + 1, chips) * 2, lax.rem(chip + chips - 1, chips) * 2

    barrier = pltpu.get_barrier_semaphore()

    def greet(to_bag, to_head):
        pl.semaphore_signal(barrier, inc=1, device_id=(to_bag, to_head), device_id_type=MESH)

    for near in (above, below):
        greet(near, head)
        greet(near + 1, head)
    greet(chip * 2 + 1 - core, head)
    for j in range(1, heads):
        greet(bag, lax.rem(head + j, heads))

    loads = [
        pltpu.make_async_copy(route_hbm, route_ref, in_sem.at[3]),
        pltpu.make_async_copy(ids_hbm, ids_ref, in_sem.at[4]),
    ] + [pltpu.make_async_copy(x_hbm.at[t], x_ref.at[t], in_sem.at[t]) for t in (1, 2, 0)]
    for load in loads:
        load.start()
    loads[0].wait()
    loads[1].wait()

    route = route_ref[...]
    lanes = jnp.broadcast_to(route.astype(F32), (tok, tok))
    down = lax.broadcasted_iota(I32, (tok, tok), 0)
    along = lax.broadcasted_iota(I32, (tok, tok), 1)
    earlier = (lanes == lanes.T) & (down < along)
    rank = jnp.sum(jnp.where(earlier, 1.0, 0.0), axis=0, keepdims=True).astype(I32)
    hit = (reach_rows(bag, down >> 1, bags) == route) & (rank == (down & 1))
    spots = jnp.where(hit, 1.0, 0.0)
    place[...] = spots.astype(BF16)
    place_t[...] = spots.T.astype(BF16)
    place_out[...] = place_t[...]

    side = mix.shape[0]
    mo = lax.broadcasted_iota(I32, (side, side), 0)
    mi = lax.broadcasted_iota(I32, (side, side), 1)
    h_bits = heads.bit_length() - 1

    def swapped(a):
        head_of, slot_of, pair_of = a >> 4, (a >> 1) & (GROUP - 1), a & 1
        return (slot_of << (h_bits + 1)) + head_of * 2 + pair_of

    mix[...] = jnp.where(swapped(mo) == mi, 1.0, 0.0).astype(BF16)
    mix_t[...] = jnp.where(swapped(mi) == mo, 1.0, 0.0).astype(BF16)

    bits = (ids_ref[...] - VIDEOS * route).astype(F32)
    row_s[...] = mat(jnp.broadcast_to(bits, (8, tok)).astype(BF16), place_t[...])[0:1]

    def split(t):
        pltpu.make_async_copy(x_hbm.at[t], x_ref.at[t], in_sem.at[t]).wait()
        picked[...] = mat(place[...], x_ref[t]).astype(BF16)

        def spread(g, carry):
            lines = pl.ds(pl.multiple_of(g * span, span), span)
            block = jnp.concatenate(
                [picked[lines, h * HD : (h + 1) * HD] for h in range(heads)], axis=0
            )
            zs[t, pl.ds(g * GROUP, GROUP)] = (
                mat(mix_t[...], block).astype(BF16).reshape(GROUP, pair, HD)
            )
            return carry

        lax.fori_loop(0, bags // GROUP, spread, 0, unroll=4)

    split(1)
    pl.semaphore_wait(barrier, 5 + heads - 1)

    def across(k, src, dst, send, recv, way):
        pltpu.make_async_remote_copy(
            src_ref=src, dst_ref=dst, send_sem=send, recv_sem=recv,
            device_id=(reach(bag, k, bags, way), head), device_id_type=MESH,
        ).start()

    def send_tensor(t, recv, lo, hi):
        def one(k, carry):
            across(k, zs.at[t, k], zr.at[t, k], zs_sem.at[t], recv, 1)
            return carry

        lax.fori_loop(lo, hi, one, 0)

    def keep(src, dst, sem):
        pltpu.make_async_copy(src, dst, sem).start()

    def arrived(ref, sem):
        pltpu.make_async_copy(ref, ref, sem).wait()

    def hand_out(src, dst, send, recv):
        def one(j, carry):
            to = lax.rem(head + 1 + j, heads)
            pltpu.make_async_remote_copy(
                src_ref=src(to), dst_ref=dst, send_sem=send, recv_sem=recv,
                device_id=(bag, to), device_id_type=MESH,
            ).start()
            return carry

        lax.fori_loop(0, heads - 1, one, 0)
        keep(src(head), dst, recv)

    hand_out(lambda to: row_s, row_r.at[head], xs_sem.at[3], xr_sem.at[2])

    send_tensor(1, zr_sem.at[0], last - 1, last)

    def widen(stage, carry):
        first_slot = 4 * (chips // 2 - stage) - 2
        for i in range(4):
            k = first_slot + i
            across(k, zs.at[1, k], zr.at[1, k], zs_sem.at[1], zr_sem.at[0], 1)
        for i, near in enumerate((below, above)):
            pl.semaphore_signal(
                wave.at[i], inc=1, device_id=(near + core, head), device_id_type=MESH
            )
        pl.semaphore_wait(wave.at[0], 1)
        pl.semaphore_wait(wave.at[1], 1)
        return carry

    lax.fori_loop(1, chips // 2, widen, 0)
    send_tensor(1, zr_sem.at[0], 0, 2)
    keep(zs.at[1, last], zr.at[1, last], zr_sem.at[0])

    share = bags // heads
    arrived(row_r, xr_sem.at[2])
    rows_in = row_r[...].reshape(heads, tok)
    odd = lax.broadcasted_iota(I32, (heads, tok), 1) & 1
    stacked = jnp.concatenate(
        [
            jnp.where(odd == 0, rows_in, 0.0),
            jnp.where(odd == 1, rows_in, 0.0),
            jnp.zeros((tok - 2 * heads, tok), F32),
        ],
        axis=0,
    )
    slot_at = lax.broadcasted_iota(I32, (bags, tok), 0)
    lane_at = lax.broadcasted_iota(I32, (bags, tok), 1)
    fold = jnp.where(slot_at == (lane_at >> 1), 1.0, 0.0)
    slot_bits = lax.dot_general(
        fold.astype(BF16), stacked.astype(BF16), (((1,), (1,)), ((), ())), preferred_element_type=F32
    )
    bit_s[...] = slot_bits.reshape(bags, 1, tok)

    def send_bits(j, carry):
        k = head + heads * j
        across(k, bit_s.at[k], bit_r.at[j], zs_sem.at[3], zr_sem.at[2], 1)
        return carry

    lax.fori_loop(0, share - 1, send_bits, 0)

    @pl.when(head < heads - 1)
    def _():
        send_bits(share - 1, 0)

    @pl.when(head == heads - 1)
    def _():
        keep(bit_s.at[last], bit_r.at[share - 1], zr_sem.at[2])

    split(2)
    send_tensor(2, zr_sem.at[1], 0, last)
    keep(zs.at[2, last], zr.at[2, last], zr_sem.at[1])
    split(0)

    def send_queries(c, carry):
        send_tensor(0, zq_sem.at[c], c * slots, (c + 1) * slots - lax.div(c, CHUNKS - 1))
        return carry

    lax.fori_loop(0, CHUNKS, send_queries, 0)
    keep(zs.at[0, last], zr.at[0, last], zq_sem.at[CHUNKS - 1])

    def gather_kv(i):
        for g in range(bags // GROUP):
            block = zr[1 + i, g * GROUP : (g + 1) * GROUP].reshape(side, HD)
            ys[i, :, g * span : (g + 1) * span, :] = (
                mat(mix[...], block).astype(BF16).reshape(heads, span, HD)
            )
        hand_out(lambda to: ys.at[i, to], kv.at[i, head], xs_sem.at[1 + i], xr_sem.at[i])

    arrived(zr.at[1], zr_sem.at[0])
    gather_kv(0)

    arrived(bit_r, zr_sem.at[2])
    hand_out(
        lambda to: bit_r, all_bits.at[pl.ds(head * share, share)], xs_sem.at[5], xr_sem.at[3]
    )
    arrived(all_bits, xr_sem.at[3])
    row_at = lax.broadcasted_iota(I32, (tok, bags), 0)
    from_at = lax.broadcasted_iota(I32, (tok, bags), 1)
    s_bits = share.bit_length() - 1
    named = (from_at >> s_bits) + heads * (from_at & (share - 1))
    wide = mat(
        jnp.where(named == (row_at >> 1), 1.0, 0.0).astype(BF16),
        all_bits[...].reshape(bags, tok).astype(BF16),
    )
    even = (lax.broadcasted_iota(I32, (tok, heads), 0) & 1) == 0
    columns = jnp.where(even, wide[:, :heads], wide[:, heads : 2 * heads])
    lane_row = lax.broadcasted_iota(I32, (1, HD), 1)
    first, second = lane_row == 0, lane_row == 1
    q_slope = jnp.where(first, 1.0, jnp.where(second, -1.0, 0.0))
    q_base = jnp.where(second, 1.0, 0.0)
    k_slope = q_slope * APART
    k_base = jnp.where(first, -APART, 0.0)
    for h in range(heads):
        column = columns[:, h : h + 1]
        qaug[:, h] = (column * q_slope + q_base).astype(BF16).reshape(CHUNKS, rows, HD)
        ka[h * tok : (h + 1) * tok, HD:] = (column * k_slope + k_base).astype(BF16)

    arrived(kv.at[0], xr_sem.at[0])
    ka[:, :HD] = kv[0].reshape(heads * tok, HD)

    arrived(zr.at[2], zr_sem.at[1])
    gather_kv(1)
    va[:, HD:] = jnp.broadcast_to(jnp.where(first, 1.0, 0.0), (heads * tok, HD)).astype(BF16)
    arrived(kv.at[1], xr_sem.at[1])
    va[:, :HD] = kv[1].reshape(heads * tok, HD)

    part = GROUP
    exponent = scaling * math.log2(math.e)

    def take(c):
        base = pl.multiple_of(c * slots, slots)
        arrived(zr.at[0, pl.ds(base, slots)], zq_sem.at[c])
        for j in range(groups):
            block = zr[0, pl.ds(base + j * GROUP, GROUP)].reshape(side, HD)
            qs[c, :, j * span : (j + 1) * span, :] = (
                mat(mix[...], block).astype(BF16).reshape(heads, span, HD)
            )
        hand_out(lambda to: qs.at[c, to], qr.at[c, head], xs_sem.at[0], xq_sem.at[c])

    take(0)

    def answer(c, carry):
        base = pl.multiple_of(c * slots, slots)
        arrived(qr.at[c], xq_sem.at[c])

        def block_of(i, inner):
            at = pl.ds(i * part, part)
            query = jnp.concatenate(
                [qr[c, at].reshape(part * rows, HD), qaug[c, at].reshape(part * rows, HD)], axis=1
            )
            scores = lax.dot_general(
                query, ka[...], (((1,), (1,)), ((), ())), preferred_element_type=F32
            )
            row_max = jnp.max(scores, axis=1, keepdims=True)
            probs = jnp.exp2((scores - row_max) * exponent).astype(BF16)
            mixed = mat(probs, va[...])
            result = (mixed[:, :HD] / mixed[:, HD : HD + 1]).astype(BF16)
            oc[c, at] = result.reshape(part, rows, HD)
            return inner

        lax.fori_loop(0, heads // part, block_of, 0)
        hand_out(lambda to: oc.at[c, to], oc_in.at[c, head], xs_sem.at[4], xo_sem.at[c])

        @pl.when(c < CHUNKS - 1)
        def _():
            take(c + 1)

        arrived(oc_in.at[c], xo_sem.at[c])
        for j in range(groups):
            block = oc_in[c, :, j * span : (j + 1) * span, :].reshape(side, HD)
            zos[pl.ds(base + j * GROUP, GROUP)] = (
                mat(mix_t[...], block).astype(BF16).reshape(GROUP, pair, HD)
            )

        def give_back(k, inner):
            across(k, zos.at[k], zor.at[k], zs_sem.at[4], zo_sem.at[c], -1)
            return inner

        lax.fori_loop(c * slots, (c + 1) * slots - lax.div(c, CHUNKS - 1), give_back, 0)
        return carry

    lax.fori_loop(0, CHUNKS, answer, 0)
    keep(zos.at[last], zor.at[last], zo_sem.at[CHUNKS - 1])

    def collect(c, carry):
        base = pl.multiple_of(c * slots, slots)
        arrived(zor.at[pl.ds(base, slots)], zo_sem.at[c])
        for j in range(groups):
            block = zor[pl.ds(base + j * GROUP, GROUP)].reshape(side, HD)
            sorted_rows = mat(mix[...], block).astype(BF16)
            for h in range(heads):
                home[c, j * span : (j + 1) * span, h * HD : (h + 1) * HD] = sorted_rows[
                    h * span : (h + 1) * span
                ]
        return carry

    lax.fori_loop(0, CHUNKS, collect, 0)

    for t in range(3):
        arrived(zs.at[t, pl.ds(0, last)], zs_sem.at[t])
    arrived(bit_s.at[pl.ds(0, share - 1)], zs_sem.at[3])

    @pl.when(head < heads - 1)
    def _():
        arrived(bit_s.at[last], zs_sem.at[3])

    arrived(zos.at[pl.ds(0, last)], zs_sem.at[4])
    arrived(qs.at[:, pl.ds(0, heads - 1)], xs_sem.at[0])
    for i in range(2):
        arrived(ys.at[i, pl.ds(0, heads - 1)], xs_sem.at[1 + i])
    arrived(row_r.at[pl.ds(0, heads - 1)], xs_sem.at[3])
    arrived(all_bits.at[pl.ds(0, bags - share)], xs_sem.at[5])
    arrived(oc.at[:, pl.ds(0, heads - 1)], xs_sem.at[4])


def local(bags, heads, projected, video_ids, bag_route):
    tok, _, feat = projected.shape
    slots = bags // CHUNKS
    rows = 2 * slots
    bag_rows = heads * tok
    side = GROUP * 2 * heads
    vm, dma = pltpu.VMEM, pltpu.SemaphoreType.DMA
    rested, order = pl.pallas_call(
        functools.partial(kernel, bags, heads, 1.0 / math.sqrt(HD)),
        out_shape=(
            jax.ShapeDtypeStruct((CHUNKS, rows, feat), BF16),
            jax.ShapeDtypeStruct((tok, tok), BF16),
        ),
        in_specs=[pl.BlockSpec(memory_space=pltpu.HBM)] * 3,
        out_specs=[pl.BlockSpec(memory_space=pltpu.VMEM)] * 2,
        scratch_shapes=[
            vm((3, tok, feat), BF16),
            vm((1, tok), I32),
            vm((1, tok), I32),
            vm((tok, tok), BF16),
            vm((tok, tok), BF16),
            vm((side, side), BF16),
            vm((side, side), BF16),
            vm((tok, feat), BF16),
            vm((3, bags, 2 * heads, HD), BF16),
            vm((3, bags, 2 * heads, HD), BF16),
            vm((2, heads, tok, HD), BF16),
            vm((2, heads, tok, HD), BF16),
            vm((CHUNKS, heads, rows, HD), BF16),
            vm((CHUNKS, heads, rows, HD), BF16),
            vm((bag_rows, 2 * HD), BF16),
            vm((bag_rows, 2 * HD), BF16),
            vm((CHUNKS, heads, rows, HD), BF16),
            vm((CHUNKS, heads, rows, HD), BF16),
            vm((CHUNKS, heads, rows, HD), BF16),
            vm((bags, 2 * heads, HD), BF16),
            vm((bags, 2 * heads, HD), BF16),
            vm((1, tok), F32),
            vm((heads, 1, tok), F32),
            vm((bags, 1, tok), F32),
            vm((bags // heads, 1, tok), F32),
            vm((bags, 1, tok), F32),
            dma((5,)),
            dma((3,)),
            dma((CHUNKS,)),
            dma((CHUNKS,)),
            dma((6,)),
            dma((4,)),
            dma((CHUNKS,)),
            dma((CHUNKS,)),
            dma((5,)),
            pltpu.SemaphoreType.REGULAR((2,)),
        ],
        compiler_params=pltpu.CompilerParams(collective_id=0, has_side_effects=True),
        name="routed_attention",
    )(jnp.transpose(projected, (1, 0, 2)), video_ids.reshape(1, tok), bag_route.reshape(1, tok))
    return mat(order, rested.reshape(tok, feat)).astype(BF16)


def solution(mesh):
    placed = (P(("bag", "head"), None, None), P(("bag", "head")), P(("bag", "head")))
    return jax.shard_map(
        functools.partial(local, mesh.shape["bag"], mesh.shape["head"]),
        mesh=mesh,
        in_specs=placed,
        out_specs=P(("bag", "head"), None),
        check_vma=False,
    )
```
